512 devices in a mesh: band: 128 (over y, x_hi, z), grid: 4 (over x_lo, core).
Axes of the slice: x: 4 (x_hi: 2, x_lo: 2; x = x_hi * 2 + x_lo), y: 4, z: 16, core: 2. Of those that a mesh axis runs over, the one named last changes fastest.
Arguments:
- bands: float32 [128, 96, 96, 96], P('band', 'grid'), may hold values from -8 to 8
Outputs:
- exchange_term: float32 [128, 96, 96, 96], P('band', 'grid')
The draws below stay inside these ranges and needn't reach their ends.
All inputs are finite; a program needn't handle non-finite values.
Results may differ from the reference program's by a relative error of at most 0.0003.
Values sent between devices are 32-bit elements; how exact they have to be, the bound alone decides.
A program may use at most 64 MiB of HBM per device.

```python
import jax
import jax.numpy as jnp
import numpy as np
from jax import lax

NX = 96
NY = 96
NZ = 96
BAND_DEV = 1
CYCLE = 2
BANDS = 128
N_BAND = 128


def draw_bands(key, part):
    full_shape = (BANDS, NX, NY, NZ)
    return jnp.clip(jax.random.normal(key, full_shape, jnp.float32), -6.0, 6.0)


def setup_inputs(seed: int = 0) -> dict:
    keys = jax.random.split(jax.random.key(seed), 2)
    bands = draw_bands(jax.random.fold_in(keys[1], 71), 0)
    return dict(bands=bands)


def wavenumber_sq(indices, length):
    folded = jnp.minimum(indices, length - indices).astype(jnp.float32)
    return (folded * (2.0 * np.pi / length)) * (folded * (2.0 * np.pi / length))


def coulomb(wave_sq, extent):
    screen = 4.0 * np.pi / extent
    guarded = jnp.where(wave_sq > 0, wave_sq, 1.0)
    screened = 0.2 * 4.0 * np.pi / guarded * (1.0 - jnp.exp(-guarded / (4.0 * screen * screen)))
    return jnp.where(wave_sq > 0, screened, 0.0)


def potential(density):
    spectrum = jnp.fft.rfftn(density, axes=(-3, -2, -1))
    wave_sq = (wavenumber_sq(jnp.arange(NX, dtype=jnp.int32), NX)[:, None, None]
               + wavenumber_sq(jnp.arange(NY, dtype=jnp.int32), NY)[None, :, None]
               + wavenumber_sq(jnp.arange(NZ // 2 + 1, dtype=jnp.int32), NZ)[None, None, :])
    return jnp.fft.irfftn(spectrum * coulomb(wave_sq, NX), s=(NX, NY, NZ), axes=(-3, -2, -1))


def reference(bands):
    def one_band(band_id):
        orbital = lax.dynamic_index_in_dim(bands, band_id, 0, keepdims=False)
        owner_block = band_id // BAND_DEV
        summed = jnp.zeros_like(orbital)
        for offset in range(-CYCLE, CYCLE + 1):
            first_row = (((owner_block + offset) % N_BAND) * BAND_DEV).astype(jnp.int32)
            partners = lax.dynamic_slice_in_dim(bands, first_row, BAND_DEV, 0)
            summed = summed + jnp.sum(potential(orbital[None] * partners) * partners, axis=0)
        return -summed

    return lax.map(one_band, jnp.arange(bands.shape[0], dtype=jnp.int32))
```

```python
import jax
import jax.numpy as jnp
import ml_dtypes
import numpy as np
from jax import lax
from jax.experimental import pallas as pl
from jax.experimental.pallas import tpu as pltpu
from jax.sharding import PartitionSpec as P

N = 96
PARTS = 4
PLANES = N // PARTS
CHUNKS = 3
DEEP = PLANES // CHUNKS
ROWS = 72
SHARE = ROWS // PARTS
LANES = 128
SCREEN = 4.0 * np.pi / N
MESH = pl.DeviceIdType.MESH
F32 = jnp.float32
BF16 = jnp.bfloat16


def tables():
    k = np.arange(N)
    angle = 2.0 * np.pi * (np.outer(k, k) % N) / N
    cas = np.cos(angle) + np.sin(angle)
    high = cas.astype(ml_dtypes.bfloat16)
    low = (cas - high.astype(np.float64)).astype(ml_dtypes.bfloat16)
    lanes = np.zeros((2 * LANES, 2 * LANES), ml_dtypes.bfloat16)
    for piece in range(2):
        lanes[piece * LANES : piece * LANES + N, :N] = high
        lanes[piece * LANES : piece * LANES + N, LANES : LANES + N] = low
    rows = np.block([[high, high], [low, low]])
    wave = (np.minimum(k, N - k) * (2.0 * np.pi / N)) ** 2
    j = np.arange(ROWS)[:, None]
    lane = np.arange(LANES)[None, :]
    first = lane < N
    ky = np.where(first, j, ROWS + j % 24)
    kz = np.where(first, lane, 32 * (j // 24) + lane - N)
    wave_yz = (wave[ky] + wave[kz]).astype(np.float32)
    wave_x = np.broadcast_to(wave[:, None], (N, LANES)).astype(np.float32)
    return lanes, rows, wave_yz, wave_x


def lane_ids(rows):
    return lax.broadcasted_iota(jnp.int32, (rows, LANES), 1)


def pack(plane):
    extra = plane[ROWS:]
    tail = lane_ids(24) >= N
    return jnp.concatenate(
        [
            jnp.where(tail, pltpu.roll(extra, N - 32 * c, 1), plane[24 * c : 24 * c + 24])
            for c in range(3)
        ],
        axis=0,
    )


def unpack(dense):
    lane = lane_ids(24)
    pieces = [pltpu.roll(dense[24 * c : 24 * c + 24], 32 * c + 32, 1) for c in range(3)]
    extra = jnp.where(lane < 32, pieces[0], jnp.where(lane < 64, pieces[1], pieces[2]))
    return jnp.concatenate([dense, extra], axis=0)


def split(x):
    high = x.astype(BF16)
    return high, (x - high.astype(F32)).astype(BF16)


def along_lanes(x, table):
    high, low = split(x)
    both = jnp.dot(
        jnp.concatenate([high, low], axis=1), table, preferred_element_type=F32
    )
    return both[:, :LANES] + both[:, LANES:]


def along_rows(x, table):
    high, low = split(x)
    both = jnp.dot(
        table, jnp.concatenate([high, low], axis=0), preferred_element_type=F32
    )
    return both[:N] + both[N:]


def exchange(
    b_ref, lanes_ref, rows_ref, wave_yz_ref, wave_x_ref, out_ref,
    own, below, above, total, coulomb,
    own_dense, below_dense, above_dense,
    to_above, to_below, from_below, from_above,
    sent, solved, back,
    local_sem, fwd_send, fwd_recv, ret_send, ret_recv,
    band_send, band_recv, term_send, term_recv,
):
    bands = lax.axis_size("band")
    me = lax.axis_index("band")
    part = lax.axis_index("grid")
    up = lax.rem(me + 1, bands)
    down = lax.rem(me + bands - 1, bands)

    barrier = pltpu.get_barrier_semaphore()
    for neighbour in (up, down):
        pl.semaphore_signal(
            barrier, inc=1, device_id={"band": neighbour}, device_id_type=MESH
        )
    for d in range(1, PARTS):
        pl.semaphore_signal(
            barrier,
            inc=1,
            device_id={"grid": lax.rem(part + d, PARTS)},
            device_id_type=MESH,
        )
    pl.semaphore_wait(barrier, PARTS + 1)

    def neighbours(k, up_src, up_dst, down_src, down_dst, send, recv):
        return (
            pltpu.make_async_remote_copy(
                up_src.at[k], up_dst.at[k], send.at[0, k], recv.at[0, k],
                device_id={"band": up}, device_id_type=MESH,
            ),
            pltpu.make_async_remote_copy(
                down_src.at[k], down_dst.at[k], send.at[1, k], recv.at[1, k],
                device_id={"band": down}, device_id_type=MESH,
            ),
        )

    def bands_out(k):
        return neighbours(
            k, own_dense, below_dense, own_dense, above_dense, band_send, band_recv
        )

    def terms_out(k):
        return neighbours(
            k, to_above, from_below, to_below, from_above, term_send, term_recv
        )

    def forward(s, k):
        copies = [
            pltpu.make_async_copy(
                sent.at[s, k, pl.ds(pl.multiple_of(part * SHARE * DEEP, 8), SHARE * DEEP)],
                solved.at[s, part * CHUNKS + k],
                local_sem.at[0, s, k],
            )
        ]
        for d in (2, 3, 1):
            peer = lax.rem(part + d, PARTS)
            copies.append(
                pltpu.make_async_remote_copy(
                    sent.at[s, k, pl.ds(pl.multiple_of(peer * SHARE * DEEP, 8), SHARE * DEEP)],
                    solved.at[s, part * CHUNKS + k],
                    fwd_send.at[s, d, k],
                    fwd_recv.at[s, d, k],
                    device_id={"grid": peer},
                    device_id_type=MESH,
                )
            )
        return copies

    def returned(s, k):
        copies = [
            pltpu.make_async_copy(
                solved.at[s, part * CHUNKS + k],
                back.at[s, k, pl.ds(pl.multiple_of(part * SHARE * DEEP, 8), SHARE * DEEP)],
                local_sem.at[1, s, k],
            )
        ]
        for d in (2, 3, 1):
            peer = lax.rem(part + d, PARTS)
            copies.append(
                pltpu.make_async_remote_copy(
                    solved.at[s, peer * CHUNKS + k],
                    back.at[s, k, pl.ds(pl.multiple_of(part * SHARE * DEEP, 8), SHARE * DEEP)],
                    ret_send.at[s, d, k],
                    ret_recv.at[s, d, k],
                    device_id={"grid": peer},
                    device_id_type=MESH,
                )
            )
        return copies

    def start(copies):
        for copy in copies:
            copy.start()

    def arrive(copies):
        copies[0].wait()
        for copy in copies[1:]:
            copy.wait_recv()

    def pairs_of_planes(body):
        lax.fori_loop(0, DEEP // 2, lambda i, c: (body(2 * i), c)[1], 0)

    def transform(s, k, i, first, second):
        z = along_lanes(jnp.concatenate([first, second], axis=0), lanes_ref[...])
        y = along_rows(jnp.concatenate([z[:N], z[N:]], axis=1), rows_ref[...])
        sent[s, k, pl.ds(i, ROWS, stride=DEEP), :] = pack(y[:, :LANES])
        sent[s, k, pl.ds(i + 1, ROWS, stride=DEEP), :] = pack(y[:, LANES:])

    def restore(s, k, i):
        first = unpack(back[s, k, pl.ds(i, ROWS, stride=DEEP), :])
        second = unpack(back[s, k, pl.ds(i + 1, ROWS, stride=DEEP), :])
        y = along_rows(jnp.concatenate([first, second], axis=1), rows_ref[...])
        return along_lanes(
            jnp.concatenate([y[:, :LANES], y[:, LANES:]], axis=0), lanes_ref[...]
        )

    def two(ref, x):
        return jnp.concatenate([ref[x], ref[x + 1]], axis=0)

    def dense_row(i):
        return pl.ds(pl.multiple_of(i * ROWS, 8), ROWS)

    for k in range(CHUNKS):

        def load(i, k=k):
            for x in (i, i + 1):
                plane = jnp.concatenate(
                    [b_ref[0, k * DEEP + x], jnp.zeros((N, LANES - N), F32)], axis=1
                )
                own[k * DEEP + x] = plane
                own_dense[k, dense_row(x), :] = pack(plane)

        pairs_of_planes(load)
        start(bands_out(k))

    for k in range(CHUNKS):

        def squared(i, k=k):
            first, second = own[k * DEEP + i], own[k * DEEP + i + 1]
            transform(0, k, i, first * first, second * second)

        pairs_of_planes(squared)
        start(forward(0, k))

    def table(j, c):
        wave_sq = wave_x_ref[...] + wave_yz_ref[pl.ds(part * SHARE + j, 1), :]
        guarded = jnp.where(wave_sq > 0, wave_sq, 1.0)
        screened = (-0.2 * 4.0 * np.pi / N**3) / guarded
        screened = screened * (1.0 - jnp.exp(guarded * (-1.0 / (4.0 * SCREEN * SCREEN))))
        coulomb[pl.ds(pl.multiple_of(j * N, 8), N), :] = jnp.where(wave_sq > 0, screened, 0.0)
        return c

    lax.fori_loop(0, SHARE, table, 0)

    for k in range(CHUNKS):
        for copy in bands_out(k):
            copy.wait_recv()

        def visitors(i, k=k):
            x = k * DEEP + i
            for e in range(2):
                above[x + e] = unpack(above_dense[k, dense_row(i + e), :])
                below[x + e] = unpack(below_dense[k, dense_row(i + e), :])
            transform(1, k, i, own[x] * above[x], own[x + 1] * above[x + 1])

        def apart(i, k=k):
            x = k * DEEP + i
            transform(2, k, i, below[x] * above[x], below[x + 1] * above[x + 1])

        pairs_of_planes(visitors)
        start(forward(1, k))
        pairs_of_planes(apart)
        start(forward(2, k))

    def solve(s):
        for k in range(CHUNKS):
            arrive(forward(s, k))

        def columns(i, c):
            at = [pl.ds(pl.multiple_of((2 * i + e) * DEEP, 8), DEEP) for e in range(2)]
            x = jnp.concatenate(
                [
                    jnp.concatenate([solved[s, p, rows, :] for p in range(N // DEEP)], axis=0)
                    for rows in at
                ],
                axis=1,
            )
            weight = jnp.concatenate(
                [
                    coulomb[pl.ds(pl.multiple_of((2 * i + e) * N, 8), N), :]
                    for e in range(2)
                ],
                axis=1,
            )
            x = along_rows(x, rows_ref[...]) * weight
            x = along_rows(x, rows_ref[...])
            for e, rows in enumerate(at):
                for p in range(N // DEEP):
                    solved[s, p, rows, :] = x[
                        p * DEEP : p * DEEP + DEEP, e * LANES : e * LANES + LANES
                    ]
            return c

        lax.fori_loop(0, SHARE // 2, columns, 0)

    solve(0)
    solve(1)
    start(returned(1, 0))
    solve(2)
    start(returned(2, 0))
    for k in range(1, CHUNKS):
        start(returned(1, k))
        start(returned(2, k))
    for k in range(CHUNKS):
        start(returned(0, k))

    for k in range(CHUNKS):
        arrive(returned(1, k))
        arrive(returned(2, k))

        def terms(i, k=k):
            x = k * DEEP + i
            near = restore(1, k, i)
            far = restore(2, k, i)
            next_band = two(above, x)
            result = near * next_band
            total[x] = result[:N]
            total[x + 1] = result[N:]
            upward = near * two(own, x) + far * two(below, x)
            downward = far * next_band
            for e in range(2):
                to_above[k, dense_row(i + e), :] = pack(upward[e * N : e * N + N])
                to_below[k, dense_row(i + e), :] = pack(downward[e * N : e * N + N])

        pairs_of_planes(terms)
        start(terms_out(k))

    for k in range(CHUNKS):
        arrive(returned(0, k))

        def same(i, k=k):
            x = k * DEEP + i
            result = restore(0, k, i) * two(own, x)
            total[x] += result[:N]
            total[x + 1] += result[N:]

        pairs_of_planes(same)

    for k in range(CHUNKS):
        for copy in terms_out(k):
            copy.wait_recv()

        def gather(i, k=k):
            for x in (i, i + 1):
                whole = (
                    total[k * DEEP + x]
                    + unpack(from_below[k, dense_row(x), :])
                    + unpack(from_above[k, dense_row(x), :])
                )
                out_ref[0, k * DEEP + x] = whole[:, :N]

        pairs_of_planes(gather)

    for k in range(CHUNKS):
        for copy in bands_out(k) + terms_out(k):
            copy.wait_send()
        for s in range(3):
            for copy in forward(s, k)[1:] + returned(s, k)[1:]:
                copy.wait_send()


def shards(bands):
    lanes, rows, wave_yz, wave_x = tables()
    vmem = pl.BlockSpec(memory_space=pltpu.VMEM)
    padded = pltpu.VMEM((PLANES, N, LANES), F32)
    dense = pltpu.VMEM((CHUNKS, DEEP * ROWS, LANES), F32)
    spectra = pltpu.VMEM((3, CHUNKS, ROWS * DEEP, LANES), F32)
    dma = pltpu.SemaphoreType.DMA
    return pl.pallas_call(
        exchange,
        out_shape=jax.ShapeDtypeStruct(bands.shape, bands.dtype),
        in_specs=[vmem] * 5,
        out_specs=vmem,
        scratch_shapes=[
            padded, padded, padded, padded,
            pltpu.VMEM((SHARE * N, LANES), F32),
            dense, dense, dense,
            dense, dense, dense, dense,
            spectra,
            pltpu.VMEM((3, N // DEEP, SHARE * DEEP, LANES), F32),
            spectra,
            dma((2, 3, CHUNKS)),
            dma((3, PARTS, CHUNKS)), dma((3, PARTS, CHUNKS)),
            dma((3, PARTS, CHUNKS)), dma((3, PARTS, CHUNKS)),
            dma((2, CHUNKS)), dma((2, CHUNKS)),
            dma((2, CHUNKS)), dma((2, CHUNKS)),
        ],
        compiler_params=pltpu.CompilerParams(
            collective_id=0, has_side_effects=True, vmem_limit_bytes=56 << 20
        ),
    )(bands, lanes, rows, wave_yz, wave_x)


def solution(mesh):
    return jax.shard_map(
        shards,
        mesh=mesh,
        in_specs=(P("band", "grid", None, None),),
        out_specs=P("band", "grid", None, None),
        check_vma=False,
    )
```

```python
import jax
import jax.numpy as jnp
import ml_dtypes
import numpy as np
from jax import lax
from jax.experimental import pallas as pl
from jax.experimental.pallas import tpu as pltpu
from jax.sharding import PartitionSpec as P

N = 96
PARTS = 4
PLANES = N // PARTS
CHUNKS = 3
DEEP = PLANES // CHUNKS
ROWS = 72
SHARE = ROWS // PARTS
LANES = 128
PIECES = DEEP // 2
COLUMN = 16
SCREEN = 4.0 * np.pi / N
MESH = pl.DeviceIdType.MESH
F32 = jnp.float32
BF16 = jnp.bfloat16


def tables():
    k = np.arange(N)
    angle = 2.0 * np.pi * (np.outer(k, k) % N) / N
    cas = np.cos(angle) + np.sin(angle)
    high = cas.astype(ml_dtypes.bfloat16)
    low = (cas - high.astype(np.float64)).astype(ml_dtypes.bfloat16)
    lanes = np.zeros((2 * LANES, 2 * LANES), ml_dtypes.bfloat16)
    for piece in range(2):
        lanes[piece * LANES : piece * LANES + N, :N] = high
        lanes[piece * LANES : piece * LANES + N, LANES : LANES + N] = low
    rows = np.block([[high, high], [low, low]])
    wave = (np.minimum(k, N - k) * (2.0 * np.pi / N)) ** 2
    j = np.arange(ROWS)[:, None]
    lane = np.arange(LANES)[None, :]
    first = lane < N
    ky = np.where(first, j, ROWS + j % 24)
    kz = np.where(first, lane, 32 * (j // 24) + lane - N)
    wave_yz = (wave[ky] + wave[kz]).astype(np.float32)
    wave_x = np.broadcast_to(wave[:, None], (N, LANES)).astype(np.float32)
    return lanes, rows, wave_yz, wave_x


def lane_ids(rows):
    return lax.broadcasted_iota(jnp.int32, (rows, LANES), 1)


def pack(plane):
    extra = plane[ROWS:]
    tail = lane_ids(24) >= N
    return jnp.concatenate(
        [
            jnp.where(tail, pltpu.roll(extra, N - 32 * c, 1), plane[24 * c : 24 * c + 24])
            for c in range(3)
        ],
        axis=0,
    )


def unpack(dense):
    lane = lane_ids(24)
    pieces = [pltpu.roll(dense[24 * c : 24 * c + 24], 32 * c + 32, 1) for c in range(3)]
    extra = jnp.where(lane < 32, pieces[0], jnp.where(lane < 64, pieces[1], pieces[2]))
    return jnp.concatenate([dense, extra], axis=0)


def split(x):
    high = x.astype(BF16)
    return high, (x - high.astype(F32)).astype(BF16)


def along_lanes(x, table):
    high, low = split(x)
    both = jnp.dot(
        jnp.concatenate([high, low], axis=1), table, preferred_element_type=F32
    )
    return both[:, :LANES] + both[:, LANES:]


def along_rows(x, table):
    high, low = split(x)
    both = jnp.dot(
        table, jnp.concatenate([high, low], axis=0), preferred_element_type=F32
    )
    return both[:N] + both[N:]


def exchange(
    b_ref, lanes_ref, rows_ref, wave_yz_ref, wave_x_ref, out_ref,
    own, visitor, total, coulomb,
    own_dense, visiting, outgoing, incoming,
    sent, solved, ready, back,
    fwd_send, fwd_recv, ret_send, ret_recv,
    band_send, band_recv, term_send, term_recv, passing, pass_send, pass_recv, here, there,
):
    bands = lax.axis_size("band")
    me = lax.axis_index("band")
    part = lax.axis_index("grid")
    level = lax.rem(me, COLUMN)
    first, last = level == 0, level == COLUMN - 1
    end = jnp.logical_or(first, last)
    host = jnp.logical_or(level == 1, level == COLUMN - 2)
    guest = jnp.where(level == 1, 0, 1)
    depth = COLUMN - 1 - level
    climbs = jnp.logical_and(level >= 2, level <= PIECES)
    sinks = jnp.logical_and(depth >= 2, depth <= PIECES)
    relays = range(2, PIECES + 1)

    def other(step):
        return {"band": lax.rem(me + step + bands, bands)}

    toward = {
        0: {"band": lax.rem(me + bands - 1, bands)},
        1: {"band": lax.rem(me + 1, bands)},
    }

    barrier = pltpu.get_barrier_semaphore()

    def greet(device):
        pl.semaphore_signal(barrier, inc=1, device_id=device, device_id_type=MESH)

    greet(toward[0])
    for d in range(1, PARTS):
        greet({"grid": lax.rem(part + d, PARTS)})

    @pl.when(jnp.logical_not(last))
    def _():
        greet(toward[1])

    @pl.when(climbs)
    def _():
        greet(other(-level - 1))

    @pl.when(sinks)
    def _():
        greet(other(depth))

    @pl.when(first)
    def _():
        for i in relays:
            greet(other(i))
            greet(other(-1 - i))

    pl.semaphore_wait(
        barrier,
        PARTS
        + jnp.where(first, 0, 1)
        + jnp.where(last, 2 * len(relays), 0)
        + jnp.where(jnp.logical_or(climbs, sinks), 1, 0),
    )

    @pl.when(last)
    def _():
        pl.semaphore_signal(here, inc=1, device_id=toward[1], device_id_type=MESH)
        for i in relays:
            pl.semaphore_signal(here, inc=1, device_id=other(-i), device_id_type=MESH)

    @pl.when(sinks)
    def _():
        pl.semaphore_signal(there, inc=1, device_id=other(depth + 1), device_id_type=MESH)

    def neighbour(k, side, src, dst, send, recv):
        return pltpu.make_async_remote_copy(
            src, dst.at[1 - side, k], send.at[side, k], recv.at[1 - side, k],
            device_id=toward[side], device_id_type=MESH,
        )

    def band_out(k, side):
        return neighbour(k, side, own_dense.at[k], visiting, band_send, band_recv)

    def term_out(k, side):
        return neighbour(k, side, outgoing.at[side, k], incoming, term_send, term_recv)

    def piece(i):
        return pl.ds(pl.multiple_of(i * 2 * ROWS, 8), 2 * ROWS)

    def term_pieces(k, side):
        way = 1 if side else -1
        return [
            pltpu.make_async_remote_copy(
                outgoing.at[side, k, piece(0)], incoming.at[1 - side, k, piece(0)],
                term_send.at[side, k], term_recv.at[1 - side, k],
                device_id=toward[side], device_id_type=MESH,
            )
        ] + [
            pltpu.make_async_remote_copy(
                outgoing.at[side, k, piece(i - 1)], passing.at[k],
                term_send.at[side, k], pass_recv.at[k],
                device_id=other(way * (1 + i)), device_id_type=MESH,
            )
            for i in relays
        ]

    def send_term(k, side):
        edge = last if side else first

        @pl.when(edge)
        def _():
            start(term_pieces(k, side))

        @pl.when(jnp.logical_not(edge))
        def _():
            term_out(k, side).start()

    def pass_on(k, side):
        at = depth if side else level
        return pltpu.make_async_remote_copy(
            passing.at[k], incoming.at[side, k, piece(at - 1)],
            pass_send.at[k], term_recv.at[side, k],
            device_id=other(depth if side else -level), device_id_type=MESH,
        )

    def pass_in(k):
        return pltpu.make_async_remote_copy(
            passing.at[k], passing.at[k], pass_send.at[k], pass_recv.at[k],
            device_id=toward[1], device_id_type=MESH,
        )

    def share(i):
        return pl.ds(pl.multiple_of(i * SHARE * DEEP, 8), SHARE * DEEP)

    def forward(s, k):
        return [
            pltpu.make_async_remote_copy(
                sent.at[s, k, share(lax.rem(part + d, PARTS))],
                solved.at[s, part * CHUNKS + k],
                fwd_send.at[s, d, k],
                fwd_recv.at[s, d, k],
                device_id={"grid": lax.rem(part + d, PARTS)},
                device_id_type=MESH,
            )
            for d in (2, 3, 1)
        ]

    def returned(s, k):
        return [
            pltpu.make_async_remote_copy(
                ready.at[s, lax.rem(part + d, PARTS) * CHUNKS + k],
                back.at[s, k, share(part)],
                ret_send.at[s, d, k],
                ret_recv.at[s, d, k],
                device_id={"grid": lax.rem(part + d, PARTS)},
                device_id_type=MESH,
            )
            for d in (2, 3, 1)
        ]

    def start(copies):
        for copy in copies:
            copy.start()

    def arrive(copies):
        for copy in copies:
            copy.wait_recv()

    def send_forward(s, k):
        start(forward(s, k))
        solved[s, part * CHUNKS + k] = sent[s, k, share(part), :]

    def send_back(s, k):
        start(returned(s, k))
        back[s, k, share(part), :] = ready[s, part * CHUNKS + k]

    def pairs_of_planes(body):
        lax.fori_loop(0, PIECES, lambda i, c: (body(i), c)[1], 0, unroll=True)

    def transform(s, k, i, first, second):
        z = along_lanes(jnp.concatenate([first, second], axis=0), lanes_ref[...])
        y = along_rows(jnp.concatenate([z[:N], z[N:]], axis=1), rows_ref[...])
        sent[s, k, pl.ds(2 * i, ROWS, stride=DEEP), :] = pack(y[:, :LANES])
        sent[s, k, pl.ds(2 * i + 1, ROWS, stride=DEEP), :] = pack(y[:, LANES:])

    def restore(s, k, i):
        first = unpack(back[s, k, pl.ds(2 * i, ROWS, stride=DEEP), :])
        second = unpack(back[s, k, pl.ds(2 * i + 1, ROWS, stride=DEEP), :])
        y = along_rows(jnp.concatenate([first, second], axis=1), rows_ref[...])
        return along_lanes(
            jnp.concatenate([y[:, :LANES], y[:, LANES:]], axis=0), lanes_ref[...]
        )

    def two(ref, *at):
        *head, x = at
        return jnp.concatenate([ref[(*head, x)], ref[(*head, x + 1)]], axis=0)

    def row(i, e):
        return pl.ds(pl.multiple_of((2 * i + e) * ROWS, 8), ROWS)

    def bring(side, k):
        band_out(k, 1 - side).wait_recv()

        def body(i):
            for e in range(2):
                visitor[side, k * DEEP + 2 * i + e] = unpack(visiting[side, k, row(i, e), :])

        pairs_of_planes(body)

    for k in range(CHUNKS):

        def load(i, k=k):
            for e in range(2):
                x = k * DEEP + 2 * i + e
                plane = jnp.concatenate(
                    [b_ref[0, x], jnp.zeros((N, LANES - N), F32)], axis=1
                )
                own[x] = plane
                own_dense[k, row(i, e), :] = pack(plane)

        pairs_of_planes(load)
        band_out(k, 1).start()

        @pl.when(jnp.logical_not(first))
        def _(k=k):
            band_out(k, 0).start()

    @pl.when(jnp.logical_not(end))
    def _():
        for k in range(CHUNKS):

            def squared(i, k=k):
                x = k * DEEP + 2 * i
                transform(0, k, i, own[x] * own[x], own[x + 1] * own[x + 1])

            pairs_of_planes(squared)
            send_forward(0, k)

    def table(j, c):
        wave_sq = wave_x_ref[...] + wave_yz_ref[pl.ds(part * SHARE + j, 1), :]
        guarded = jnp.where(wave_sq > 0, wave_sq, 1.0)
        screened = (-0.2 * 4.0 * np.pi / N**3) / guarded
        screened = screened * (1.0 - jnp.exp(guarded * (-1.0 / (4.0 * SCREEN * SCREEN))))
        coulomb[pl.ds(pl.multiple_of(j * N, 8), N), :] = jnp.where(wave_sq > 0, screened, 0.0)
        return c

    lax.fori_loop(0, SHARE, table, 0)

    for k in range(CHUNKS):
        bring(1, k)

        def beside(i, k=k):
            x = k * DEEP + 2 * i
            transform(1, k, i, own[x] * visitor[1, x], own[x + 1] * visitor[1, x + 1])

        pairs_of_planes(beside)
        send_forward(1, k)
        if k == 0:

            @pl.when(first)
            def _():
                pl.semaphore_wait(here, 1)
                for late in range(CHUNKS):
                    band_out(late, 0).start()

    for k in range(CHUNKS):
        bring(0, k)

        def apart(i, k=k):
            x = k * DEEP + 2 * i
            transform(
                2, k, i, visitor[0, x] * visitor[1, x], visitor[0, x + 1] * visitor[1, x + 1]
            )

        pairs_of_planes(apart)
        send_forward(2, k)

    @pl.when(host)
    def _():
        for k in range(CHUNKS):

            def squared(i, k=k):
                x = k * DEEP + 2 * i
                one, other = visitor[guest, x], visitor[guest, x + 1]
                transform(3, k, i, one * one, other * other)

            pairs_of_planes(squared)
            send_forward(3, k)

    def solve(s):
        for k in range(CHUNKS):
            arrive(forward(s, k))

        def columns(i, c):
            at = [pl.ds(pl.multiple_of((2 * i + e) * DEEP, 8), DEEP) for e in range(2)]
            x = jnp.concatenate(
                [
                    jnp.concatenate([solved[s, p, rows, :] for p in range(N // DEEP)], axis=0)
                    for rows in at
                ],
                axis=1,
            )
            weight = jnp.concatenate(
                [
                    coulomb[pl.ds(pl.multiple_of((2 * i + e) * N, 8), N), :]
                    for e in range(2)
                ],
                axis=1,
            )
            x = along_rows(x, rows_ref[...]) * weight
            x = along_rows(x, rows_ref[...])
            for e, rows in enumerate(at):
                for p in range(N // DEEP):
                    ready[s, p, rows, :] = x[
                        p * DEEP : p * DEEP + DEEP, e * LANES : e * LANES + LANES
                    ]
            return c

        lax.fori_loop(0, SHARE // 2, columns, 0, unroll=3)

    @pl.when(jnp.logical_not(end))
    def _():
        solve(0)

    solve(1)
    send_back(1, 0)
    solve(2)
    send_back(2, 0)
    send_back(1, 1)

    @pl.when(host)
    def _():
        solve(3)
        send_back(3, 0)

    send_back(2, 1)
    send_back(1, 2)

    @pl.when(host)
    def _():
        send_back(3, 1)

    send_back(2, 2)

    @pl.when(host)
    def _():
        send_back(3, 2)

    @pl.when(jnp.logical_not(end))
    def _():
        for k in range(CHUNKS):
            send_back(0, k)

    for k in range(CHUNKS):
        arrive(returned(1, k))
        arrive(returned(2, k))

        def terms(i, k=k):
            x = k * DEEP + 2 * i
            near = restore(1, k, i)
            far = restore(2, k, i)
            next_band = two(visitor, 1, x)
            result = near * next_band
            total[x] = result[:N]
            total[x + 1] = result[N:]
            upward = near * two(own, x) + far * two(visitor, 0, x)
            downward = far * next_band
            for e in range(2):
                outgoing[1, k, row(i, e), :] = pack(upward[e * N : e * N + N])
                outgoing[0, k, row(i, e), :] = pack(downward[e * N : e * N + N])

        pairs_of_planes(terms)

        @pl.when(host)
        def _(k=k):
            arrive(returned(3, k))

            def theirs(i):
                result = restore(3, k, i) * two(visitor, guest, k * DEEP + 2 * i)
                for e in range(2):
                    outgoing[guest, k, row(i, e), :] += pack(result[e * N : e * N + N])

            pairs_of_planes(theirs)

        if k == 0:

            @pl.when(first)
            def _():
                pl.semaphore_wait(there, len(relays))

        send_term(k, 1)
        send_term(k, 0)

    @pl.when(jnp.logical_not(end))
    def _():
        for k in range(CHUNKS):
            arrive(returned(0, k))

            def same(i, k=k):
                x = k * DEEP + 2 * i
                result = restore(0, k, i) * two(own, x)
                total[x] += result[:N]
                total[x + 1] += result[N:]

            pairs_of_planes(same)

    @pl.when(climbs)
    def _():
        for k in range(CHUNKS):
            pass_in(k).wait_recv()
            pass_on(k, 0).start()

    @pl.when(sinks)
    def _():
        pl.semaphore_wait(here, 1)
        for k in range(CHUNKS):
            pass_in(k).wait_recv()
            pass_on(k, 1).start()

    for k in range(CHUNKS):
        term_out(k, 1).wait_recv()
        term_out(k, 0).wait_recv()

        def gather(i, k=k):
            for e in range(2):
                x = k * DEEP + 2 * i + e
                whole = (
                    total[x]
                    + unpack(incoming[0, k, row(i, e), :])
                    + unpack(incoming[1, k, row(i, e), :])
                )
                out_ref[0, x] = whole[:, :N]

        pairs_of_planes(gather)

    def gone(s):
        for k in range(CHUNKS):
            for copy in forward(s, k) + returned(s, k):
                copy.wait_send()

    for k in range(CHUNKS):
        for side in range(2):
            band_out(k, side).wait_send()
            term_out(k, side).wait_send()
    gone(1)
    gone(2)

    @pl.when(jnp.logical_not(end))
    def _():
        gone(0)

    @pl.when(host)
    def _():
        gone(3)

    @pl.when(jnp.logical_or(climbs, sinks))
    def _():
        for k in range(CHUNKS):
            pass_in(k).wait_send()


def shards(bands):
    lanes, rows, wave_yz, wave_x = tables()
    vmem = pl.BlockSpec(memory_space=pltpu.VMEM)
    padded = pltpu.VMEM((PLANES, N, LANES), F32)
    dense = pltpu.VMEM((CHUNKS, DEEP * ROWS, LANES), F32)
    both = pltpu.VMEM((2, CHUNKS, DEEP * ROWS, LANES), F32)
    spectra = pltpu.VMEM((4, CHUNKS, ROWS * DEEP, LANES), F32)
    columns = pltpu.VMEM((4, N // DEEP, SHARE * DEEP, LANES), F32)
    dma = pltpu.SemaphoreType.DMA
    exchanged = dma((4, PARTS, CHUNKS))
    sides = dma((2, CHUNKS))
    return pl.pallas_call(
        exchange,
        out_shape=jax.ShapeDtypeStruct(bands.shape, bands.dtype),
        in_specs=[vmem] * 5,
        out_specs=vmem,
        scratch_shapes=[
            padded, pltpu.VMEM((2, PLANES, N, LANES), F32), padded,
            pltpu.VMEM((SHARE * N, LANES), F32),
            dense, both, both, both,
            spectra, columns, columns, spectra,
            exchanged, exchanged, exchanged, exchanged,
            sides, sides, sides, sides,
            pltpu.VMEM((CHUNKS, 2 * ROWS, LANES), F32), dma((CHUNKS,)), dma((CHUNKS,)),
            pltpu.SemaphoreType.REGULAR, pltpu.SemaphoreType.REGULAR,
        ],
        compiler_params=pltpu.CompilerParams(
            collective_id=0, has_side_effects=True, vmem_limit_bytes=56 << 20
        ),
    )(bands, lanes, rows, wave_yz, wave_x)


def solution(mesh):
    return jax.shard_map(
        shards,
        mesh=mesh,
        in_specs=(P("band", "grid", None, None),),
        out_specs=P("band", "grid", None, None),
        check_vma=False,
    )
```

```python
import jax
import jax.numpy as jnp
import ml_dtypes
import numpy as np
from jax import lax
from jax.experimental import pallas as pl
from jax.experimental.pallas import tpu as pltpu
from jax.sharding import PartitionSpec as P

N = 96
PARTS = 4
PLANES = N // PARTS
CHUNKS = 3
DEEP = PLANES // CHUNKS
ROWS = 72
SHARE = ROWS // PARTS
LANES = 128
PIECES = DEEP // 2
COLUMN = 16
SCREEN = 4.0 * np.pi / N
MESH = pl.DeviceIdType.MESH
F32 = jnp.float32
BF16 = jnp.bfloat16


def tables():
    k = np.arange(N)
    angle = 2.0 * np.pi * (np.outer(k, k) % N) / N
    cas = np.cos(angle) + np.sin(angle)
    high = cas.astype(ml_dtypes.bfloat16)
    low = (cas - high.astype(np.float64)).astype(ml_dtypes.bfloat16)
    lanes = np.zeros((2 * LANES, 2 * LANES), ml_dtypes.bfloat16)
    for piece in range(2):
        lanes[piece * LANES : piece * LANES + N, :N] = high
        lanes[piece * LANES : piece * LANES + N, LANES : LANES + N] = low
    rows = np.block([[high, high], [low, low]])
    wave = (np.minimum(k, N - k) * (2.0 * np.pi / N)) ** 2
    j = np.arange(ROWS)[:, None]
    lane = np.arange(LANES)[None, :]
    first = lane < N
    ky = np.where(first, j, ROWS + j % 24)
    kz = np.where(first, lane, 32 * (j // 24) + lane - N)
    wave_yz = (wave[ky] + wave[kz]).astype(np.float32)
    wave_x = np.broadcast_to(wave[:, None], (N, LANES)).astype(np.float32)
    return lanes, rows, wave_yz, wave_x


def lane_ids(rows):
    return lax.broadcasted_iota(jnp.int32, (rows, LANES), 1)


def pack(plane):
    extra = plane[ROWS:]
    tail = lane_ids(24) >= N
    return jnp.concatenate(
        [
            jnp.where(tail, pltpu.roll(extra, N - 32 * c, 1), plane[24 * c : 24 * c + 24])
            for c in range(3)
        ],
        axis=0,
    )


def unpack(dense):
    lane = lane_ids(24)
    pieces = [pltpu.roll(dense[24 * c : 24 * c + 24], 32 * c + 32, 1) for c in range(3)]
    extra = jnp.where(lane < 32, pieces[0], jnp.where(lane < 64, pieces[1], pieces[2]))
    return jnp.concatenate([dense, extra], axis=0)


def split(x):
    high = x.astype(BF16)
    return high, (x - high.astype(F32)).astype(BF16)


def along_lanes(x, table):
    high, low = split(x)
    both = jnp.dot(
        jnp.concatenate([high, low], axis=1), table, preferred_element_type=F32
    )
    return both[:, :LANES] + both[:, LANES:]


def along_rows(x, table):
    high, low = split(x)
    both = jnp.dot(
        table, jnp.concatenate([high, low], axis=0), preferred_element_type=F32
    )
    return both[:N] + both[N:]


def exchange(
    b_ref, lanes_ref, rows_ref, wave_yz_ref, wave_x_ref, out_ref,
    own, visitor, total, coulomb,
    own_dense, visiting, outgoing, incoming,
    sent, solved, ready, back,
    fwd_send, fwd_recv, ret_send, ret_recv,
    band_send, band_recv, term_send, term_recv, here,
):
    bands = lax.axis_size("band")
    me = lax.axis_index("band")
    part = lax.axis_index("grid")
    level = lax.rem(me, COLUMN)
    first, last = level == 0, level == COLUMN - 1
    mate = jnp.where(level < COLUMN // 2, 0, 1)
    host = level == 1
    middle = level == COLUMN // 2 - 1
    third = jnp.logical_or(host, middle)

    def unless(condition):
        return pl.when(jnp.logical_not(condition))

    toward = {
        0: {"band": lax.rem(me + bands - 1, bands)},
        1: {"band": lax.rem(me + 1, bands)},
    }

    barrier = pltpu.get_barrier_semaphore()

    def greet(device):
        pl.semaphore_signal(barrier, inc=1, device_id=device, device_id_type=MESH)

    greet(toward[0])
    for d in range(1, PARTS):
        greet({"grid": lax.rem(part + d, PARTS)})

    @pl.when(jnp.logical_not(last))
    def _():
        greet(toward[1])

    pl.semaphore_wait(barrier, jnp.where(first, PARTS, PARTS + 1))

    @pl.when(last)
    def _():
        pl.semaphore_signal(here, inc=1, device_id=toward[1], device_id_type=MESH)

    def neighbour(k, side, src, dst, send, recv):
        return pltpu.make_async_remote_copy(
            src, dst.at[1 - side, k], send.at[side, k], recv.at[1 - side, k],
            device_id=toward[side], device_id_type=MESH,
        )

    def band_out(k, side):
        return neighbour(k, side, own_dense.at[k], visiting, band_send, band_recv)

    def term_out(k, side):
        return neighbour(k, side, outgoing.at[side, k], incoming, term_send, term_recv)

    def share(i):
        return pl.ds(pl.multiple_of(i * SHARE * DEEP, 8), SHARE * DEEP)

    def forward(s, k):
        return [
            pltpu.make_async_remote_copy(
                sent.at[s, k, share(lax.rem(part + d, PARTS))],
                solved.at[s, part * CHUNKS + k],
                fwd_send.at[s, d, k],
                fwd_recv.at[s, d, k],
                device_id={"grid": lax.rem(part + d, PARTS)},
                device_id_type=MESH,
            )
            for d in (2, 3, 1)
        ]

    def returned(s, k):
        return [
            pltpu.make_async_remote_copy(
                ready.at[s, lax.rem(part + d, PARTS) * CHUNKS + k],
                back.at[s, k, share(part)],
                ret_send.at[s, d, k],
                ret_recv.at[s, d, k],
                device_id={"grid": lax.rem(part + d, PARTS)},
                device_id_type=MESH,
            )
            for d in (2, 3, 1)
        ]

    def start(copies):
        for copy in copies:
            copy.start()

    def arrive(copies):
        for copy in copies:
            copy.wait_recv()

    def send_forward(s, k):
        start(forward(s, k))
        solved[s, part * CHUNKS + k] = sent[s, k, share(part), :]

    def send_back(s, k):
        start(returned(s, k))
        back[s, k, share(part), :] = ready[s, part * CHUNKS + k]

    def pairs_of_planes(body):
        lax.fori_loop(0, PIECES, lambda i, c: (body(i), c)[1], 0, unroll=True)

    def transform(s, k, i, first, second):
        z = along_lanes(jnp.concatenate([first, second], axis=0), lanes_ref[...])
        y = along_rows(jnp.concatenate([z[:N], z[N:]], axis=1), rows_ref[...])
        sent[s, k, pl.ds(2 * i, ROWS, stride=DEEP), :] = pack(y[:, :LANES])
        sent[s, k, pl.ds(2 * i + 1, ROWS, stride=DEEP), :] = pack(y[:, LANES:])

    def restore(s, k, i):
        first = unpack(back[s, k, pl.ds(2 * i, ROWS, stride=DEEP), :])
        second = unpack(back[s, k, pl.ds(2 * i + 1, ROWS, stride=DEEP), :])
        y = along_rows(jnp.concatenate([first, second], axis=1), rows_ref[...])
        return along_lanes(
            jnp.concatenate([y[:, :LANES], y[:, LANES:]], axis=0), lanes_ref[...]
        )

    def two(ref, *at):
        *head, x = at
        return jnp.concatenate([ref[(*head, x)], ref[(*head, x + 1)]], axis=0)

    def row(i, e):
        return pl.ds(pl.multiple_of((2 * i + e) * ROWS, 8), ROWS)

    def bring(side, k):
        pltpu.make_async_remote_copy(
            own_dense.at[k], visiting.at[side, k], band_send.at[0, k], band_recv.at[side, k],
            device_id=toward[1], device_id_type=MESH,
        ).wait_recv()

        def body(i):
            for e in range(2):
                visitor[side, k * DEEP + 2 * i + e] = unpack(visiting[side, k, row(i, e), :])

        pairs_of_planes(body)

    def alone(k):
        def squared(i):
            x = k * DEEP + 2 * i
            transform(0, k, i, own[x] * own[x], own[x + 1] * own[x + 1])

        pairs_of_planes(squared)
        send_forward(0, k)

    for k in range(CHUNKS):

        def load(i, k=k):
            for e in range(2):
                x = k * DEEP + 2 * i + e
                plane = jnp.concatenate(
                    [b_ref[0, x], jnp.zeros((N, LANES - N), F32)], axis=1
                )
                own[x] = plane
                own_dense[k, row(i, e), :] = pack(plane)

        pairs_of_planes(load)
        band_out(k, 1).start()

        @pl.when(jnp.logical_not(first))
        def _(k=k):
            band_out(k, 0).start()

    @pl.when(first)
    def _():
        pl.semaphore_wait(here, 1)
        for k in range(CHUNKS):
            band_out(k, 0).start()

    @unless(jnp.logical_or(first, last))
    def _():
        for k in range(CHUNKS):
            alone(k)

    def table(j, c):
        wave_sq = wave_x_ref[...] + wave_yz_ref[pl.ds(part * SHARE + j, 1), :]
        guarded = jnp.where(wave_sq > 0, wave_sq, 1.0)
        screened = (-0.2 * 4.0 * np.pi / N**3) / guarded
        screened = screened * (1.0 - jnp.exp(guarded * (-1.0 / (4.0 * SCREEN * SCREEN))))
        coulomb[pl.ds(pl.multiple_of(j * N, 8), N), :] = jnp.where(wave_sq > 0, screened, 0.0)
        return c

    lax.fori_loop(0, SHARE, table, 0)

    @unless(last)
    def _():
        for k in range(CHUNKS):
            bring(mate, k)

            def beside(i, k=k):
                x = k * DEEP + 2 * i
                transform(
                    1, k, i, own[x] * visitor[mate, x], own[x + 1] * visitor[mate, x + 1]
                )

            pairs_of_planes(beside)
            send_forward(1, k)

    for k in range(CHUNKS):

        @pl.when(last)
        def _(k=k):
            bring(1, k)

        bring(1 - mate, k)

        def apart(i, k=k):
            x = k * DEEP + 2 * i
            transform(
                2, k, i, visitor[0, x] * visitor[1, x], visitor[0, x + 1] * visitor[1, x + 1]
            )

        pairs_of_planes(apart)
        send_forward(2, k)

    @pl.when(host)
    def _():
        for k in range(CHUNKS):

            def guest(i, k=k):
                x = k * DEEP + 2 * i
                one, other = visitor[0, x], visitor[0, x + 1]
                transform(3, k, i, one * one, other * other)

            pairs_of_planes(guest)
            send_forward(3, k)

    @pl.when(middle)
    def _():
        for k in range(CHUNKS):

            def bridge(i, k=k):
                x = k * DEEP + 2 * i
                transform(3, k, i, own[x] * visitor[1, x], own[x + 1] * visitor[1, x + 1])

            pairs_of_planes(bridge)
            send_forward(3, k)

    @pl.when(last)
    def _():
        for k in range(CHUNKS):
            alone(k)

    def solve(s):
        for k in range(CHUNKS):
            arrive(forward(s, k))

        def columns(i, c):
            at = [pl.ds(pl.multiple_of((2 * i + e) * DEEP, 8), DEEP) for e in range(2)]
            x = jnp.concatenate(
                [
                    jnp.concatenate([solved[s, p, rows, :] for p in range(N // DEEP)], axis=0)
                    for rows in at
                ],
                axis=1,
            )
            weight = jnp.concatenate(
                [
                    coulomb[pl.ds(pl.multiple_of((2 * i + e) * N, 8), N), :]
                    for e in range(2)
                ],
                axis=1,
            )
            x = along_rows(x, rows_ref[...]) * weight
            x = along_rows(x, rows_ref[...])
            for e, rows in enumerate(at):
                for p in range(N // DEEP):
                    ready[s, p, rows, :] = x[
                        p * DEEP : p * DEEP + DEEP, e * LANES : e * LANES + LANES
                    ]
            return c

        lax.fori_loop(0, SHARE // 2, columns, 0, unroll=3)

    @unless(jnp.logical_or(first, last))
    def _():
        solve(0)

    @unless(last)
    def _():
        solve(1)
        send_back(1, 0)

    solve(2)
    send_back(2, 0)

    @unless(last)
    def _():
        send_back(1, 1)

    @pl.when(third)
    def _():
        solve(3)
        send_back(3, 0)

    send_back(2, 1)

    @unless(last)
    def _():
        send_back(1, 2)

    @pl.when(third)
    def _():
        send_back(3, 1)

    send_back(2, 2)

    @pl.when(third)
    def _():
        send_back(3, 2)

    @pl.when(last)
    def _():
        solve(0)

    @unless(first)
    def _():
        for k in range(CHUNKS):
            send_back(0, k)

    upper = jnp.where(mate == 1, 1.0, 0.0).astype(F32)

    def put(side, k, i, planes, add=False):
        for e in range(2):
            dense = pack(planes[e * N : e * N + N])
            if add:
                dense = dense + outgoing[side, k, row(i, e), :]
            outgoing[side, k, row(i, e), :] = dense

    for k in range(CHUNKS):
        arrive(returned(2, k))

        @unless(last)
        def _(k=k):
            arrive(returned(1, k))

            def terms(i):
                x = k * DEEP + 2 * i
                near = restore(1, k, i)
                far = restore(2, k, i)
                result = near * two(visitor, mate, x)
                total[x] = result[:N]
                total[x + 1] = result[N:]
                near = near * two(own, x)
                put(1, k, i, far * two(visitor, 0, x) + near * upper)
                put(0, k, i, far * two(visitor, 1, x) + near * (1.0 - upper))

            pairs_of_planes(terms)

        @pl.when(last)
        def _(k=k):
            def terms(i):
                x = k * DEEP + 2 * i
                far = restore(2, k, i)
                total[x] = jnp.zeros((N, LANES), F32)
                total[x + 1] = jnp.zeros((N, LANES), F32)
                put(1, k, i, far * two(visitor, 0, x))
                put(0, k, i, far * two(visitor, 1, x))

            pairs_of_planes(terms)

        @pl.when(host)
        def _(k=k):
            arrive(returned(3, k))

            def theirs(i):
                put(0, k, i, restore(3, k, i) * two(visitor, 0, k * DEEP + 2 * i), add=True)

            pairs_of_planes(theirs)

        @pl.when(middle)
        def _(k=k):
            arrive(returned(3, k))

            def across(i):
                x = k * DEEP + 2 * i
                near = restore(3, k, i)
                result = near * two(visitor, 1, x)
                total[x] += result[:N]
                total[x + 1] += result[N:]
                put(1, k, i, near * two(own, x), add=True)

            pairs_of_planes(across)

        term_out(k, 1).start()
        term_out(k, 0).start()

    @unless(first)
    def _():
        for k in range(CHUNKS):
            arrive(returned(0, k))

            def same(i, k=k):
                x = k * DEEP + 2 * i
                result = restore(0, k, i) * two(own, x)
                total[x] += result[:N]
                total[x + 1] += result[N:]

            pairs_of_planes(same)

    for k in range(CHUNKS):
        term_out(k, 1).wait_recv()
        term_out(k, 0).wait_recv()

        def gather(i, k=k):
            for e in range(2):
                x = k * DEEP + 2 * i + e
                whole = (
                    total[x]
                    + unpack(incoming[0, k, row(i, e), :])
                    + unpack(incoming[1, k, row(i, e), :])
                )
                out_ref[0, x] = whole[:, :N]

        pairs_of_planes(gather)

    def gone(s):
        for k in range(CHUNKS):
            for copy in forward(s, k) + returned(s, k):
                copy.wait_send()

    for k in range(CHUNKS):
        for side in range(2):
            band_out(k, side).wait_send()
            term_out(k, side).wait_send()
    gone(2)

    @unless(last)
    def _():
        gone(1)

    @unless(first)
    def _():
        gone(0)

    @pl.when(third)
    def _():
        gone(3)


def shards(bands):
    lanes, rows, wave_yz, wave_x = tables()
    vmem = pl.BlockSpec(memory_space=pltpu.VMEM)
    padded = pltpu.VMEM((PLANES, N, LANES), F32)
    dense = pltpu.VMEM((CHUNKS, DEEP * ROWS, LANES), F32)
    both = pltpu.VMEM((2, CHUNKS, DEEP * ROWS, LANES), F32)
    spectra = pltpu.VMEM((4, CHUNKS, ROWS * DEEP, LANES), F32)
    columns = pltpu.VMEM((4, N // DEEP, SHARE * DEEP, LANES), F32)
    dma = pltpu.SemaphoreType.DMA
    exchanged = dma((4, PARTS, CHUNKS))
    sides = dma((2, CHUNKS))
    return pl.pallas_call(
        exchange,
        out_shape=jax.ShapeDtypeStruct(bands.shape, bands.dtype),
        in_specs=[vmem] * 5,
        out_specs=vmem,
        scratch_shapes=[
            padded, pltpu.VMEM((2, PLANES, N, LANES), F32), padded,
            pltpu.VMEM((SHARE * N, LANES), F32),
            dense, both, both, both,
            spectra, columns, columns, spectra,
            exchanged, exchanged, exchanged, exchanged,
            sides, sides, sides, sides,
            pltpu.SemaphoreType.REGULAR,
        ],
        compiler_params=pltpu.CompilerParams(
            collective_id=0, has_side_effects=True, vmem_limit_bytes=56 << 20
        ),
    )(bands, lanes, rows, wave_yz, wave_x)


def solution(mesh):
    return jax.shard_map(
        shards,
        mesh=mesh,
        in_specs=(P("band", "grid", None, None),),
        out_specs=P("band", "grid", None, None),
        check_vma=False,
    )
```

```python
import jax
import jax.numpy as jnp
import ml_dtypes
import numpy as np
from jax import lax
from jax.experimental import pallas as pl
from jax.experimental.pallas import tpu as pltpu
from jax.sharding import PartitionSpec as P

N = 96
PARTS = 4
PLANES = N // PARTS
CHUNKS = 3
DEEP = PLANES // CHUNKS
ROWS = 72
SHARE = ROWS // PARTS
LANES = 128
PIECES = DEEP // 2
COLUMN = 16
SCREEN = 4.0 * np.pi / N
MESH = pl.DeviceIdType.MESH
F32 = jnp.float32
BF16 = jnp.bfloat16


def tables():
    k = np.arange(N)
    angle = 2.0 * np.pi * (np.outer(k, k) % N) / N
    cas = np.cos(angle) + np.sin(angle)
    high = cas.astype(ml_dtypes.bfloat16)
    low = (cas - high.astype(np.float64)).astype(ml_dtypes.bfloat16)
    lanes = np.zeros((2 * LANES, 2 * LANES), ml_dtypes.bfloat16)
    for piece in range(2):
        lanes[piece * LANES : piece * LANES + N, :N] = high
        lanes[piece * LANES : piece * LANES + N, LANES : LANES + N] = low
    rows = np.block([[high, high], [low, low]])
    wave = (np.minimum(k, N - k) * (2.0 * np.pi / N)) ** 2
    j = np.arange(ROWS)[:, None]
    lane = np.arange(LANES)[None, :]
    first = lane < N
    ky = np.where(first, j, ROWS + j % 24)
    kz = np.where(first, lane, 32 * (j // 24) + lane - N)
    wave_yz = (wave[ky] + wave[kz]).astype(np.float32)
    wave_x = np.broadcast_to(wave[:, None], (N, LANES)).astype(np.float32)
    return lanes, rows, wave_yz, wave_x


def lane_ids(rows):
    return lax.broadcasted_iota(jnp.int32, (rows, LANES), 1)


def pack(plane):
    extra = plane[ROWS:]
    tail = lane_ids(24) >= N
    return jnp.concatenate(
        [
            jnp.where(tail, pltpu.roll(extra, N - 32 * c, 1), plane[24 * c : 24 * c + 24])
            for c in range(3)
        ],
        axis=0,
    )


def unpack(dense):
    lane = lane_ids(24)
    pieces = [pltpu.roll(dense[24 * c : 24 * c + 24], 32 * c + 32, 1) for c in range(3)]
    extra = jnp.where(lane < 32, pieces[0], jnp.where(lane < 64, pieces[1], pieces[2]))
    return jnp.concatenate([dense, extra], axis=0)


def split(x):
    high = x.astype(BF16)
    return high, (x - high.astype(F32)).astype(BF16)


def along_lanes(x, table):
    high, low = split(x)
    both = jnp.dot(
        jnp.concatenate([high, low], axis=1), table, preferred_element_type=F32
    )
    return both[:, :LANES] + both[:, LANES:]


def along_rows(x, table):
    high, low = split(x)
    both = jnp.dot(
        table, jnp.concatenate([high, low], axis=0), preferred_element_type=F32
    )
    return both[:N] + both[N:]


def exchange(
    b_ref, lanes_ref, rows_ref, wave_yz_ref, wave_x_ref, out_ref,
    own, visitor, total, coulomb,
    own_dense, visiting, outgoing, incoming,
    sent, solved, ready, back,
    fwd_send, fwd_recv, ret_send, ret_recv,
    band_send, band_recv, term_send, term_recv, here,
):
    bands = lax.axis_size("band")
    me = lax.axis_index("band")
    part = lax.axis_index("grid")
    level = lax.rem(me, COLUMN)
    first, last = level == 0, level == COLUMN - 1
    mate = jnp.where(level < COLUMN // 2, 0, 1)
    host = level == 1
    middle = level == COLUMN // 2 - 1
    third = jnp.logical_or(host, middle)

    def unless(condition):
        return pl.when(jnp.logical_not(condition))

    toward = {
        0: {"band": lax.rem(me + bands - 1, bands)},
        1: {"band": lax.rem(me + 1, bands)},
    }

    barrier = pltpu.get_barrier_semaphore()

    def greet(device):
        pl.semaphore_signal(barrier, inc=1, device_id=device, device_id_type=MESH)

    greet(toward[0])
    for d in range(1, PARTS):
        greet({"grid": lax.rem(part + d, PARTS)})

    @pl.when(jnp.logical_not(last))
    def _():
        greet(toward[1])

    pl.semaphore_wait(barrier, jnp.where(first, PARTS, PARTS + 1))

    @pl.when(last)
    def _():
        pl.semaphore_signal(here, inc=1, device_id=toward[1], device_id_type=MESH)

    def neighbour(k, side, src, dst, send, recv):
        return pltpu.make_async_remote_copy(
            src, dst.at[1 - side, k], send.at[side, k], recv.at[1 - side, k],
            device_id=toward[side], device_id_type=MESH,
        )

    def band_out(k, side):
        return neighbour(k, side, own_dense.at[k], visiting, band_send, band_recv)

    def term_out(k, side):
        return neighbour(k, side, outgoing.at[side, k], incoming, term_send, term_recv)

    def share(i):
        return pl.ds(pl.multiple_of(i * SHARE * DEEP, 8), SHARE * DEEP)

    def forward(s, k):
        return [
            pltpu.make_async_remote_copy(
                sent.at[s, k, share(lax.rem(part + d, PARTS))],
                solved.at[s, part * CHUNKS + k],
                fwd_send.at[s, d, k],
                fwd_recv.at[s, d, k],
                device_id={"grid": lax.rem(part + d, PARTS)},
                device_id_type=MESH,
            )
            for d in (2, 3, 1)
        ]

    def returned(s, k):
        return [
            pltpu.make_async_remote_copy(
                ready.at[s, lax.rem(part + d, PARTS) * CHUNKS + k],
                back.at[s, k, share(part)],
                ret_send.at[s, d, k],
                ret_recv.at[s, d, k],
                device_id={"grid": lax.rem(part + d, PARTS)},
                device_id_type=MESH,
            )
            for d in (2, 3, 1)
        ]

    def start(copies):
        for copy in copies:
            copy.start()

    def arrive(copies):
        for copy in copies:
            copy.wait_recv()

    def send_forward(s, k):
        start(forward(s, k))
        solved[s, part * CHUNKS + k] = sent[s, k, share(part), :]

    def send_back(s, k):
        start(returned(s, k))
        back[s, k, share(part), :] = ready[s, part * CHUNKS + k]

    def pairs_of_planes(body):
        lax.fori_loop(0, PIECES, lambda i, c: (body(i), c)[1], 0, unroll=True)

    def transform(s, k, i, first, second):
        z = along_lanes(jnp.concatenate([first, second], axis=0), lanes_ref[...])
        y = along_rows(jnp.concatenate([z[:N], z[N:]], axis=1), rows_ref[...])
        sent[s, k, pl.ds(2 * i, ROWS, stride=DEEP), :] = pack(y[:, :LANES])
        sent[s, k, pl.ds(2 * i + 1, ROWS, stride=DEEP), :] = pack(y[:, LANES:])

    def restore(s, k, i):
        first = unpack(back[s, k, pl.ds(2 * i, ROWS, stride=DEEP), :])
        second = unpack(back[s, k, pl.ds(2 * i + 1, ROWS, stride=DEEP), :])
        y = along_rows(jnp.concatenate([first, second], axis=1), rows_ref[...])
        return along_lanes(
            jnp.concatenate([y[:, :LANES], y[:, LANES:]], axis=0), lanes_ref[...]
        )

    def two(ref, *at):
        *head, x = at
        return jnp.concatenate([ref[(*head, x)], ref[(*head, x + 1)]], axis=0)

    def row(i, e):
        return pl.ds(pl.multiple_of((2 * i + e) * ROWS, 8), ROWS)

    def bring(side, k):
        pltpu.make_async_remote_copy(
            own_dense.at[k], visiting.at[side, k], band_send.at[0, k], band_recv.at[side, k],
            device_id=toward[1], device_id_type=MESH,
        ).wait_recv()

        def body(i):
            for e in range(2):
                visitor[side, k * DEEP + 2 * i + e] = unpack(visiting[side, k, row(i, e), :])

        pairs_of_planes(body)

    def alone(k):
        def squared(i):
            x = k * DEEP + 2 * i
            transform(0, k, i, own[x] * own[x], own[x + 1] * own[x + 1])

        pairs_of_planes(squared)
        send_forward(0, k)

    for k in range(CHUNKS):

        def load(i, k=k):
            for e in range(2):
                x = k * DEEP + 2 * i + e
                plane = jnp.concatenate(
                    [b_ref[0, x], jnp.zeros((N, LANES - N), F32)], axis=1
                )
                own[x] = plane
                own_dense[k, row(i, e), :] = pack(plane)

        pairs_of_planes(load)
        band_out(k, 1).start()

        @pl.when(jnp.logical_not(first))
        def _(k=k):
            band_out(k, 0).start()

    @pl.when(first)
    def _():
        pl.semaphore_wait(here, 1)
        for k in range(CHUNKS):
            band_out(k, 0).start()

    @unless(jnp.logical_or(first, last))
    def _():
        for k in range(CHUNKS):
            alone(k)

    def table(j, c):
        wave_sq = wave_x_ref[...] + wave_yz_ref[pl.ds(part * SHARE + j, 1), :]
        guarded = jnp.where(wave_sq > 0, wave_sq, 1.0)
        screened = (-0.2 * 4.0 * np.pi / N**3) / guarded
        screened = screened * (1.0 - jnp.exp(guarded * (-1.0 / (4.0 * SCREEN * SCREEN))))
        coulomb[pl.ds(pl.multiple_of(j * N, 8), N), :] = jnp.where(wave_sq > 0, screened, 0.0)
        return c

    lax.fori_loop(0, SHARE, table, 0)

    @unless(last)
    def _():
        for k in range(CHUNKS):
            bring(mate, k)

            def beside(i, k=k):
                x = k * DEEP + 2 * i
                transform(
                    1, k, i, own[x] * visitor[mate, x], own[x + 1] * visitor[mate, x + 1]
                )

            pairs_of_planes(beside)
            send_forward(1, k)

    for k in range(CHUNKS):

        @pl.when(last)
        def _(k=k):
            bring(1, k)

        bring(1 - mate, k)

        def apart(i, k=k):
            x = k * DEEP + 2 * i
            transform(
                2, k, i, visitor[0, x] * visitor[1, x], visitor[0, x + 1] * visitor[1, x + 1]
            )

        pairs_of_planes(apart)
        send_forward(2, k)

    @pl.when(host)
    def _():
        for k in range(CHUNKS):

            def guest(i, k=k):
                x = k * DEEP + 2 * i
                one, other = visitor[0, x], visitor[0, x + 1]
                transform(3, k, i, one * one, other * other)

            pairs_of_planes(guest)
            send_forward(3, k)

    @pl.when(middle)
    def _():
        for k in range(CHUNKS):

            def bridge(i, k=k):
                x = k * DEEP + 2 * i
                transform(3, k, i, own[x] * visitor[1, x], own[x + 1] * visitor[1, x + 1])

            pairs_of_planes(bridge)
            send_forward(3, k)

    def solve(s):
        for k in range(CHUNKS):
            arrive(forward(s, k))

        def columns(i, c):
            at = [pl.ds(pl.multiple_of((2 * i + e) * DEEP, 8), DEEP) for e in range(2)]
            x = jnp.concatenate(
                [
                    jnp.concatenate([solved[s, p, rows, :] for p in range(N // DEEP)], axis=0)
                    for rows in at
                ],
                axis=1,
            )
            weight = jnp.concatenate(
                [
                    coulomb[pl.ds(pl.multiple_of((2 * i + e) * N, 8), N), :]
                    for e in range(2)
                ],
                axis=1,
            )
            x = along_rows(x, rows_ref[...]) * weight
            x = along_rows(x, rows_ref[...])
            for e, rows in enumerate(at):
                for p in range(N // DEEP):
                    ready[s, p, rows, :] = x[
                        p * DEEP : p * DEEP + DEEP, e * LANES : e * LANES + LANES
                    ]
            return c

        lax.fori_loop(0, SHARE // 2, columns, 0, unroll=3)

    @unless(jnp.logical_or(first, last))
    def _():
        solve(0)

    @unless(last)
    def _():
        solve(1)
        send_back(1, 0)

    solve(2)
    send_back(2, 0)

    @unless(last)
    def _():
        send_back(1, 1)

    @pl.when(third)
    def _():
        solve(3)
        send_back(3, 0)

    send_back(2, 1)

    @unless(last)
    def _():
        send_back(1, 2)

    @pl.when(third)
    def _():
        send_back(3, 1)

    send_back(2, 2)

    @pl.when(third)
    def _():
        send_back(3, 2)

    @pl.when(last)
    def _():
        for k in range(CHUNKS):
            alone(k)
        solve(0)

    @unless(first)
    def _():
        for k in range(CHUNKS):
            send_back(0, k)

    upper = jnp.where(mate == 1, 1.0, 0.0).astype(F32)

    def put(side, k, i, planes, add=False):
        for e in range(2):
            dense = pack(planes[e * N : e * N + N])
            if add:
                dense = dense + outgoing[side, k, row(i, e), :]
            outgoing[side, k, row(i, e), :] = dense

    for k in range(CHUNKS):
        arrive(returned(2, k))

        @unless(last)
        def _(k=k):
            arrive(returned(1, k))

            def terms(i):
                x = k * DEEP + 2 * i
                near = restore(1, k, i)
                far = restore(2, k, i)
                result = near * two(visitor, mate, x)
                total[x] = result[:N]
                total[x + 1] = result[N:]
                near = near * two(own, x)
                put(1, k, i, far * two(visitor, 0, x) + near * upper)
                put(0, k, i, far * two(visitor, 1, x) + near * (1.0 - upper))

            pairs_of_planes(terms)

        @pl.when(last)
        def _(k=k):
            def terms(i):
                x = k * DEEP + 2 * i
                far = restore(2, k, i)
                total[x] = jnp.zeros((N, LANES), F32)
                total[x + 1] = jnp.zeros((N, LANES), F32)
                put(1, k, i, far * two(visitor, 0, x))
                put(0, k, i, far * two(visitor, 1, x))

            pairs_of_planes(terms)

        @pl.when(host)
        def _(k=k):
            arrive(returned(3, k))

            def theirs(i):
                put(0, k, i, restore(3, k, i) * two(visitor, 0, k * DEEP + 2 * i), add=True)

            pairs_of_planes(theirs)

        @pl.when(middle)
        def _(k=k):
            arrive(returned(3, k))

            def across(i):
                x = k * DEEP + 2 * i
                near = restore(3, k, i)
                result = near * two(visitor, 1, x)
                total[x] += result[:N]
                total[x + 1] += result[N:]
                put(1, k, i, near * two(own, x), add=True)

            pairs_of_planes(across)

        term_out(k, 1).start()
        term_out(k, 0).start()

    @unless(first)
    def _():
        for k in range(CHUNKS):
            arrive(returned(0, k))

            def same(i, k=k):
                x = k * DEEP + 2 * i
                result = restore(0, k, i) * two(own, x)
                total[x] += result[:N]
                total[x + 1] += result[N:]

            pairs_of_planes(same)

    for k in range(CHUNKS):
        term_out(k, 1).wait_recv()
        term_out(k, 0).wait_recv()

        def gather(i, k=k):
            for e in range(2):
                x = k * DEEP + 2 * i + e
                whole = (
                    total[x]
                    + unpack(incoming[0, k, row(i, e), :])
                    + unpack(incoming[1, k, row(i, e), :])
                )
                out_ref[0, x] = whole[:, :N]

        pairs_of_planes(gather)

    def gone(s):
        for k in range(CHUNKS):
            for copy in forward(s, k) + returned(s, k):
                copy.wait_send()

    for k in range(CHUNKS):
        for side in range(2):
            band_out(k, side).wait_send()
            term_out(k, side).wait_send()
    gone(2)

    @unless(last)
    def _():
        gone(1)

    @unless(first)
    def _():
        gone(0)

    @pl.when(third)
    def _():
        gone(3)


def shards(bands):
    lanes, rows, wave_yz, wave_x = tables()
    vmem = pl.BlockSpec(memory_space=pltpu.VMEM)
    padded = pltpu.VMEM((PLANES, N, LANES), F32)
    dense = pltpu.VMEM((CHUNKS, DEEP * ROWS, LANES), F32)
    both = pltpu.VMEM((2, CHUNKS, DEEP * ROWS, LANES), F32)
    spectra = pltpu.VMEM((4, CHUNKS, ROWS * DEEP, LANES), F32)
    columns = pltpu.VMEM((4, N // DEEP, SHARE * DEEP, LANES), F32)
    dma = pltpu.SemaphoreType.DMA
    exchanged = dma((4, PARTS, CHUNKS))
    sides = dma((2, CHUNKS))
    return pl.pallas_call(
        exchange,
        out_shape=jax.ShapeDtypeStruct(bands.shape, bands.dtype),
        in_specs=[vmem] * 5,
        out_specs=vmem,
        scratch_shapes=[
            padded, pltpu.VMEM((2, PLANES, N, LANES), F32), padded,
            pltpu.VMEM((SHARE * N, LANES), F32),
            dense, both, both, both,
            spectra, columns, columns, spectra,
            exchanged, exchanged, exchanged, exchanged,
            sides, sides, sides, sides,
            pltpu.SemaphoreType.REGULAR,
        ],
        compiler_params=pltpu.CompilerParams(
            collective_id=0, has_side_effects=True, vmem_limit_bytes=56 << 20
        ),
    )(bands, lanes, rows, wave_yz, wave_x)


def solution(mesh):
    return jax.shard_map(
        shards,
        mesh=mesh,
        in_specs=(P("band", "grid", None, None),),
        out_specs=P("band", "grid", None, None),
        check_vma=False,
    )
```
